32 devices in a mesh: frame: 2 (over core), slab: 16 (over z, y, x).
Axes of the slice: x: 2, y: 2, z: 4, core: 2. Of those that a mesh axis runs over, the one named last changes fastest.
Arguments:
- volume: float32 [2, 1024, 8192], P('frame', 'slab'), may hold values from -6 to 6
- measured: float32 [2, 2, 1024, 8192], P('frame', None, None, 'slab'), may hold values from -6 to 6
- cutoff: int32 [2, 8192], P('frame', 'slab'), may hold values from 128 to 384
Outputs:
- smoothed: float32 [2, 1024, 8192], P('frame', 'slab')
The draws below stay inside these ranges and needn't reach their ends.
All inputs are finite; a program needn't handle non-finite values.
Results may differ from the reference program's by a relative error of at most 0.0003.
Values sent between devices are 32-bit elements; how exact they have to be, the bound alone decides.
No kernel may reach another device: no remote copies, remote signals or barrier semaphores. Data moves between devices by JAX's collectives and lax.ppermute only.
A program may use at most 128 MiB of HBM per device.

```python
import jax
import jax.numpy as jnp
from jax import lax

NZ = 1024
PIX = 8192
FRAMES = 2


def set_ends(array, stream_key, smallest, high):
    place = [jax.random.randint(jax.random.fold_in(stream_key, axis), (), 0, length) for axis, length in enumerate(array.shape)]
    longest = array.shape.index(max(array.shape))
    beside = place[:longest] + [(place[longest] + 1) % array.shape[longest]] + place[longest + 1:]
    return array.at[tuple(place)].set(smallest).at[tuple(beside)].set(high)


def shard_levels(stream_key, extent, cuts, low, largest):
    gain = 1.0
    for position, shards_of in cuts:
        heights = jax.random.uniform(jax.random.fold_in(jax.random.fold_in(stream_key, 6), position), (shards_of,), jnp.float32, low / len(cuts), largest / len(cuts))
        gain = gain * jnp.repeat(jnp.exp(heights), extent[position] // shards_of).reshape((-1,) + (1,) * (len(extent) - 1 - position))
    return gain


def scatter_about(stream_key, extent, spread, limit, split=(), held_as=jnp.bfloat16):
    values = jax.random.normal(stream_key, extent, jnp.float32) * spread
    if len(split) > 0:
        values = shard_levels(stream_key, extent, split, -0.22, 0.18) * values
    return jnp.clip(values, min=-limit, max=limit).astype(held_as)


def setup_inputs(seed: int = 0) -> dict:
    streams_of = jax.random.split(jax.random.key(seed), 4)
    volume = scatter_about(streams_of[0], (FRAMES, NZ, PIX), 1.0, 6.0, ((0, 2), (1, 16)), jnp.float32)
    measured = scatter_about(streams_of[1], (FRAMES, 2, NZ, PIX), 1.0, 6.0, ((0, 2), (3, 16)), jnp.float32)
    cutoff = set_ends(jax.random.randint(streams_of[2], (FRAMES, PIX), NZ // 8, 3 * NZ // 8 + 1), jax.random.fold_in(streams_of[2], 1), NZ // 8, (3 * NZ // 8 + 1) - 1).astype(jnp.int32)
    return dict(volume=volume, measured=measured, cutoff=cutoff)


tv_step_size = 0.25
tv_weight = 1.0

def tv_step(extended, anchor, first_frame, frames):
    difference = extended[1:] - extended[:-1]
    frame_ids = first_frame + jnp.arange(difference.shape[0], dtype=jnp.int32)
    inside = ((frame_ids >= 0) & (frame_ids <= frames - 2))[:, None, None]
    fluxes = jnp.where(inside, difference / jnp.sqrt(difference * difference + 1.0), 0.0)
    interior = extended[1:-1]
    return interior - tv_step_size * (interior - anchor + tv_weight * (fluxes[:-1] - fluxes[1:]))

def transform_frame(packed):
    column_field, spectrum, limits = packed
    scale = jnp.sqrt(jnp.float32(NZ))
    forward = jnp.fft.fft(column_field, axis=0)
    real_part = jnp.real(forward) / scale
    imag_part = jnp.imag(forward) / scale
    indices = jnp.arange(NZ, dtype=jnp.int32)
    signed = jnp.where(indices < NZ // 2, indices, indices - NZ)
    measured_mask = jnp.abs(signed)[:, None] <= limits[None, :]
    real_part = jnp.where(measured_mask, spectrum[0], real_part)
    imag_part = jnp.where(measured_mask, spectrum[1], imag_part)
    backward = jnp.fft.ifft(lax.complex(real_part, imag_part), axis=0)
    return jnp.real(backward) * scale

def reference(volume, measured, cutoff):
    anchor = lax.map(transform_frame, (volume, measured, cutoff))
    current = anchor
    for step in range(2):
        extended = jnp.pad(current, ((1, 1), (0, 0), (0, 0)))
        current = tv_step(extended, anchor, -1, FRAMES)
    return current
```

```python
import functools
import math

import jax
import jax.numpy as jnp
import numpy as np
from jax import lax
from jax.experimental import pallas as pl
from jax.experimental.pallas import tpu as pltpu
from jax.sharding import PartitionSpec as P

tv_step_size = 0.25
tv_weight = 1.0
EXTRA = 8


def split(array):
    high = array.astype(jnp.bfloat16)
    low = (array - high.astype(jnp.float32)).astype(jnp.bfloat16)
    return high, low


def product(table_high, table_low, array):
    high, low = split(array)
    dot = functools.partial(jnp.dot, preferred_element_type=jnp.float32)
    return dot(table_high[...], high) + (dot(table_high[...], low) + dot(table_low[...], high))


def as_pair(table):
    table = table.astype(np.float32)
    high = table.astype(jnp.bfloat16)
    low = (table - high.astype(np.float32)).astype(jnp.bfloat16)
    return [jnp.asarray(high), jnp.asarray(low)]


def rows(length, first, count):
    k = first + 2 * np.arange(count)
    z = np.arange(length // 2)
    angle = (k[:, None] * z[None, :] % length) * (2.0 * math.pi / length)
    table = np.concatenate([np.cos(angle), -np.sin(angle)], axis=0) / math.sqrt(length)
    return k, table


def band_tables(length):
    count = 3 * length // 16
    result = []
    for first in (length // 8 + 2, length // 8 + 1):
        k, table = rows(length, first, count)
        weight = np.where(k == length // 2, 1.0, 2.0)
        result += as_pair(table * np.concatenate([weight, weight])[:, None])
        result += as_pair(table.T)
    return result


def measured_tables(length):
    result = []
    for first in (0, 1):
        result += as_pair(rows(length, first, length // 2)[1].T)
    return result


def measured_kernel(measured, cutoff, even_high, even_low, odd_high, odd_low, out):
    length = measured.shape[1]
    half = length // 2
    limit = cutoff[...]
    parts = []
    for first, high, low in ((0, even_high, even_low), (1, odd_high, odd_low)):
        k = first + 2 * lax.broadcasted_iota(jnp.int32, (half, limit.shape[1]), 0)
        keep = jnp.where(k < half, k, length - k) <= limit
        stacked = [
            jnp.where(keep, measured[part, pl.ds(first, half, stride=2), :], 0.0) for part in (0, 1)
        ]
        parts.append(product(high, low, jnp.concatenate(stacked, axis=0)))
    out[:half, :] = parts[0] + parts[1]
    out[half:length, :] = parts[0] - parts[1]
    out[length:, :] = jnp.broadcast_to(limit.astype(jnp.float32), (EXTRA, limit.shape[1]))


def measured_part(measured, cutoff, tables):
    length, columns = measured.shape[1:]
    width = 128 if columns % 128 == 0 else columns
    whole = pl.BlockSpec(memory_space=pltpu.VMEM)
    return pl.pallas_call(
        measured_kernel,
        grid=(columns // width,),
        in_specs=[
            pl.BlockSpec((2, length, width), lambda i: (0, 0, i)),
            pl.BlockSpec((1, width), lambda i: (0, i)),
        ]
        + [whole] * len(tables),
        out_specs=pl.BlockSpec((length + EXTRA, width), lambda i: (0, i)),
        out_shape=jax.ShapeDtypeStruct((length + EXTRA, columns), jnp.float32),
        name="measured_part",
    )(measured, cutoff, *tables)


def restore_kernel(mine, columns, *refs):
    frames, length, width = columns.shape
    known = refs[:frames]
    feh, fel, ieh, iel, foh, fol, ioh, iol, out = refs[frames:]
    half = length // 2
    count = feh.shape[0] // 2
    for shift in range(frames):
        f = lax.rem(mine[0] + frames - shift, frames)
        low = columns[f, :half, :]
        high = columns[f, half:, :]
        limit = known[shift][length : length + 1, :]
        parts = []
        for first, field, tables in (
            (length // 8 + 2, low + high, (feh, fel, ieh, iel)),
            (length // 8 + 1, low - high, (foh, fol, ioh, iol)),
        ):
            spectrum = product(tables[0], tables[1], field)
            index = lax.broadcasted_iota(jnp.int32, spectrum.shape, 0)
            k = first + 2 * jnp.where(index < count, index, index - count)
            spectrum = jnp.where(k.astype(jnp.float32) > limit, spectrum, 0.0)
            parts.append(product(tables[2], tables[3], spectrum))
        out[f, :half, :] = known[shift][:half, :] + (parts[0] + parts[1])
        out[f, half:, :] = known[shift][half:length, :] + (parts[0] - parts[1])

    block = 32

    def smooth(i, carry):
        at = pl.ds(pl.multiple_of(i * block, block), block)
        anchor = [out[f, at, :] for f in range(frames)]
        current = anchor
        for _ in range(2):
            fluxes = []
            for f in range(frames - 1):
                d = current[f + 1] - current[f]
                fluxes.append(d * lax.rsqrt(d * d + 1.0))
            following = []
            for f in range(frames):
                flow = 0.0
                if f > 0:
                    flow = flow + fluxes[f - 1]
                if f < frames - 1:
                    flow = flow - fluxes[f]
                following.append(
                    current[f] - tv_step_size * ((current[f] - anchor[f]) + tv_weight * flow)
                )
            current = following
        for f in range(frames):
            out[f, at, :] = current[f]
        return carry

    lax.fori_loop(0, length // block, smooth, 0)


def restore(mine, columns, known, tables):
    whole = pl.BlockSpec(memory_space=pltpu.VMEM)
    return pl.pallas_call(
        restore_kernel,
        in_specs=[pl.BlockSpec(memory_space=pltpu.SMEM)] + [whole] * (1 + len(known) + len(tables)),
        out_specs=whole,
        out_shape=jax.ShapeDtypeStruct(columns.shape, jnp.float32),
        name="restore",
    )(mine, columns, *known, *tables)


def pack_kernel(field, out, sems):
    teams, slabs, _, width = out.shape
    copies = []
    for t in range(teams):
        for s in range(slabs):
            at = pl.ds((s * teams + t) * width, width)
            copies.append(
                pltpu.make_async_copy(field.at[:, at], out.at[t, s], sems.at[t * slabs + s])
            )
    for copy in copies:
        copy.start()
    for copy in copies:
        copy.wait()


def pack(field, teams, slabs):
    planes, pixels = field.shape
    width = pixels // (teams * slabs)
    if width % 128:
        return field.reshape(planes, slabs, teams, width).transpose(2, 1, 0, 3)
    return pl.pallas_call(
        pack_kernel,
        in_specs=[pl.BlockSpec(memory_space=pl.ANY)],
        out_specs=pl.BlockSpec(memory_space=pltpu.VMEM),
        out_shape=jax.ShapeDtypeStruct((teams, slabs, planes, width), jnp.float32),
        scratch_shapes=[pltpu.SemaphoreType.DMA((teams * slabs,))],
        name="pack",
    )(field)


def unpack_kernel(parts, out, sems):
    teams, slabs, _, width = parts.shape
    copies = []
    for t in range(teams):
        for s in range(slabs):
            at = pl.ds((s * teams + t) * width, width)
            copies.append(
                pltpu.make_async_copy(parts.at[t, s], out.at[:, at], sems.at[t * slabs + s])
            )
    for copy in copies:
        copy.start()
    for copy in copies:
        copy.wait()


def unpack(parts):
    teams, slabs, planes, width = parts.shape
    if width % 128:
        return parts.transpose(2, 1, 0, 3).reshape(planes, teams * slabs * width)
    return pl.pallas_call(
        unpack_kernel,
        in_specs=[pl.BlockSpec(memory_space=pltpu.VMEM)],
        out_specs=pl.BlockSpec(memory_space=pl.ANY),
        out_shape=jax.ShapeDtypeStruct((planes, teams * slabs * width), jnp.float32),
        scratch_shapes=[pltpu.SemaphoreType.DMA((teams * slabs,))],
        name="unpack",
    )(parts)


def on_device(volume, measured, cutoff):
    _, planes, pixels = volume.shape
    teams = lax.axis_size("frame")
    slabs = lax.axis_size("slab")
    mine = lax.axis_index("frame")
    length = planes * slabs
    width = pixels // (teams * slabs)
    axes = ("frame", "slab")

    sent = pack(volume[0], teams, slabs).reshape(teams * slabs, planes, width)
    columns = lax.all_to_all(sent, axes, split_axis=0, concat_axis=0, tiled=True)

    known = []
    own_tables = measured_tables(length)
    for shift in range(teams - 1, -1, -1):
        start = lax.rem(mine + shift, teams) * width
        part = measured_part(
            lax.dynamic_slice_in_dim(measured[0], start, width, axis=2),
            lax.dynamic_slice_in_dim(cutoff, start, width, axis=1),
            own_tables,
        )
        if shift:
            part = lax.ppermute(part, "frame", [(t, (t + shift) % teams) for t in range(teams)])
        known.insert(0, part)

    done = restore(
        mine.reshape(1), columns.reshape(teams, length, width), known, band_tables(length)
    )
    done = done.reshape(teams * slabs, planes, width)
    done = lax.all_to_all(done, axes, split_axis=0, concat_axis=0, tiled=True)
    return unpack(done.reshape(teams, slabs, planes, width))[None]


def solution(mesh):
    placed = (P("frame", "slab", None), P("frame", None, None, "slab"), P("frame", "slab"))
    return jax.shard_map(
        on_device, mesh=mesh, in_specs=placed, out_specs=P("frame", "slab", None), check_vma=False
    )
```

```python
import functools
import math

import jax
import jax.numpy as jnp
import numpy as np
from jax import lax
from jax.experimental import pallas as pl
from jax.experimental.pallas import tpu as pltpu
from jax.sharding import PartitionSpec as P

tv_step_size = 0.25
tv_weight = 1.0
EXTRA = 8


def split(array):
    high = array.astype(jnp.bfloat16)
    low = (array - high.astype(jnp.float32)).astype(jnp.bfloat16)
    return high, low


def product(table_high, table_low, array):
    high, low = split(array)
    dot = functools.partial(jnp.dot, preferred_element_type=jnp.float32)
    return dot(table_high[...], high) + (dot(table_high[...], low) + dot(table_low[...], high))


def in_vmem(array):
    return pltpu.with_memory_space_constraint(array, pltpu.VMEM)


def in_hbm(array):
    return pltpu.with_memory_space_constraint(array, pltpu.HBM)


def as_pair(table):
    table = table.astype(np.float32)
    high = table.astype(jnp.bfloat16)
    low = (table - high.astype(np.float32)).astype(jnp.bfloat16)
    return [jnp.asarray(high), jnp.asarray(low)]


def rows(length, first, count):
    k = first + 2 * np.arange(count)
    z = np.arange(length // 2)
    angle = (k[:, None] * z[None, :] % length) * (2.0 * math.pi / length)
    table = np.concatenate([np.cos(angle), -np.sin(angle)], axis=0) / math.sqrt(length)
    return k, table


def band_tables(length):
    count = 3 * length // 16
    result = []
    for first in (length // 8 + 2, length // 8 + 1):
        k, table = rows(length, first, count)
        weight = np.where(k == length // 2, 1.0, 2.0)
        result += as_pair(table * np.concatenate([weight, weight])[:, None])
        result += as_pair(table.T)
    return result


def measured_tables(length):
    result = []
    for first in (0, 1):
        result += as_pair(rows(length, first, length // 2)[1].T)
    return result


def measured_kernel(measured, cutoff, even_high, even_low, odd_high, odd_low, out):
    length = measured.shape[1]
    half = length // 2
    limit = cutoff[...]
    parts = []
    for first, high, low in ((0, even_high, even_low), (1, odd_high, odd_low)):
        k = first + 2 * lax.broadcasted_iota(jnp.int32, (half, limit.shape[1]), 0)
        keep = jnp.where(k < half, k, length - k) <= limit
        stacked = [
            jnp.where(keep, measured[part, pl.ds(first, half, stride=2), :], 0.0) for part in (0, 1)
        ]
        parts.append(product(high, low, jnp.concatenate(stacked, axis=0)))
    out[:half, :] = parts[0] + parts[1]
    out[half:length, :] = parts[0] - parts[1]
    out[length:, :] = jnp.broadcast_to(limit.astype(jnp.float32), (EXTRA, limit.shape[1]))


def measured_part(measured, cutoff, tables):
    length, columns = measured.shape[1:]
    width = 128 if columns % 128 == 0 else columns
    whole = pl.BlockSpec(memory_space=pltpu.VMEM)
    return pl.pallas_call(
        measured_kernel,
        grid=(columns // width,),
        in_specs=[
            pl.BlockSpec((2, length, width), lambda i: (0, 0, i)),
            pl.BlockSpec((1, width), lambda i: (0, i)),
        ]
        + [whole] * len(tables),
        out_specs=pl.BlockSpec((length + EXTRA, width), lambda i: (0, i)),
        out_shape=jax.ShapeDtypeStruct((length + EXTRA, columns), jnp.float32),
        compiler_params=pltpu.CompilerParams(vmem_limit_bytes=32 * 1024 * 1024),
        name="measured_part",
    )(measured, cutoff, *[in_vmem(table) for table in tables])


def restore_kernel(mine, columns, *refs):
    slabs, frames, planes, width = columns.shape
    length = slabs * planes
    fetched = refs[frames + 2 : frames + 8]
    out = refs[frames + 8]
    known, sems = refs[-2:]
    tables = refs[frames : frames + 2] + refs[frames + 9 : -2]
    table_copies = [
        pltpu.make_async_copy(table, copy, sems.at[frames + i])
        for i, (table, copy) in enumerate(zip(fetched, tables[2:]))
    ]
    known_copies = [
        pltpu.make_async_copy(refs[shift], known.at[shift], sems.at[shift])
        for shift in range(frames)
    ]
    for copy in table_copies + known_copies:
        copy.start()
    half = length // 2
    count = tables[0].shape[0] // 2
    where = [lax.rem(mine[0] + frames - shift, frames) for shift in range(frames)]
    parts = []
    for side, first in ((0, length // 8 + 2), (1, length // 8 + 1)):
        index = lax.broadcasted_iota(jnp.int32, (2 * count, width), 0)
        k = (first + 2 * jnp.where(index < count, index, index - count)).astype(jnp.float32)
        if side == 1:
            for copy in table_copies[2:4]:
                copy.wait()
        spectra = []
        for f in where:
            low = columns[: slabs // 2, f].reshape(half, width)
            high = columns[slabs // 2 :, f].reshape(half, width)
            field = low + high if side == 0 else low - high
            spectra.append(product(tables[4 * side], tables[4 * side + 1], field))
        if side == 0:
            for copy in table_copies[:2] + known_copies:
                copy.wait()
        else:
            for copy in table_copies[4:]:
                copy.wait()
        for shift in range(frames):
            limit = known[shift, length : length + 1, :]
            spectrum = jnp.where(k > limit, spectra[shift], 0.0)
            parts.append(product(tables[4 * side + 2], tables[4 * side + 3], spectrum))
    for shift, f in enumerate(where):
        even, odd = parts[shift], parts[frames + shift]
        low = known[shift, :half, :] + (even + odd)
        high = known[shift, half:length, :] + (even - odd)
        out[: slabs // 2, f] = low.reshape(slabs // 2, planes, width)
        out[slabs // 2 :, f] = high.reshape(slabs // 2, planes, width)

    def smooth(i, carry):
        anchor = [out[i, f] for f in range(frames)]
        current = anchor
        for _ in range(2):
            fluxes = []
            for f in range(frames - 1):
                d = current[f + 1] - current[f]
                fluxes.append(d * lax.rsqrt(d * d + 1.0))
            following = []
            for f in range(frames):
                flow = 0.0
                if f > 0:
                    flow = flow + fluxes[f - 1]
                if f < frames - 1:
                    flow = flow - fluxes[f]
                following.append(
                    current[f] - tv_step_size * ((current[f] - anchor[f]) + tv_weight * flow)
                )
            current = following
        for f in range(frames):
            out[i, f] = current[f]
        return carry

    lax.fori_loop(0, slabs, smooth, 0)


def restore(mine, columns, known, tables):
    whole = pl.BlockSpec(memory_space=pltpu.VMEM)
    return pl.pallas_call(
        restore_kernel,
        in_specs=[pl.BlockSpec(memory_space=pltpu.SMEM), whole]
        + [pl.BlockSpec(memory_space=pltpu.HBM)] * len(known)
        + [whole] * 2
        + [pl.BlockSpec(memory_space=pltpu.HBM)] * (len(tables) - 2),
        out_specs=whole,
        out_shape=pltpu.VMEM(columns.shape, jnp.float32),
        scratch_shapes=[pltpu.VMEM(table.shape, table.dtype) for table in tables[2:]]
        + [
            pltpu.VMEM((len(known),) + known[0].shape, jnp.float32),
            pltpu.SemaphoreType.DMA((len(known) + len(tables),)),
        ],
        compiler_params=pltpu.CompilerParams(vmem_limit_bytes=24 * 1024 * 1024),
        name="restore",
    )(
        mine,
        in_vmem(columns),
        *map(in_hbm, known),
        *map(in_vmem, tables[:2]),
        *map(in_hbm, tables[2:]),
    )


def pack_kernel(field, out, rows, held, here, there):
    strips, strip, _ = rows.shape
    devices, _, width = out.shape
    at = [pl.ds(i * strip, strip) for i in range(strips)]
    loads = [
        pltpu.make_async_copy(field.at[at[i], :], rows.at[i], here.at[i]) for i in range(strips)
    ]
    stores = [
        pltpu.make_async_copy(held.at[i], out.at[:, at[i], :], there.at[i]) for i in range(strips)
    ]
    for load in loads:
        load.start()
    for i in range(strips):
        loads[i].wait()
        for d in range(devices):
            held[i, d] = rows[i, :, d * width : (d + 1) * width]
        stores[i].start()
    for store in stores:
        store.wait()


def pack(field, devices):
    planes, pixels = field.shape
    width = pixels // devices
    if width % 128:
        return field.reshape(planes, devices, width).transpose(1, 0, 2)
    strips = planes // 16
    return pl.pallas_call(
        pack_kernel,
        in_specs=[pl.BlockSpec(memory_space=pltpu.HBM)],
        out_specs=pl.BlockSpec(memory_space=pltpu.HBM),
        out_shape=pltpu.HBM((devices, planes, width), jnp.float32),
        scratch_shapes=[
            pltpu.VMEM((strips, 16, pixels), jnp.float32),
            pltpu.VMEM((strips, devices, 16, width), jnp.float32),
            pltpu.SemaphoreType.DMA((strips,)),
            pltpu.SemaphoreType.DMA((strips,)),
        ],
        compiler_params=pltpu.CompilerParams(vmem_limit_bytes=8 * 1024 * 1024),
        name="pack",
    )(in_hbm(field))


def unpack_kernel(parts, out, sems):
    devices, _, width = parts.shape
    copies = [
        pltpu.make_async_copy(parts.at[i], out.at[:, pl.ds(i * width, width)], sems.at[i])
        for i in range(devices)
    ]
    for copy in copies:
        copy.start()
    for copy in copies:
        copy.wait()


def unpack(parts):
    devices, planes, width = parts.shape
    if width % 128:
        return parts.transpose(1, 0, 2).reshape(planes, devices * width)
    return pl.pallas_call(
        unpack_kernel,
        in_specs=[pl.BlockSpec(memory_space=pltpu.VMEM)],
        out_specs=pl.BlockSpec(memory_space=pltpu.HBM),
        out_shape=jax.ShapeDtypeStruct((planes, devices * width), jnp.float32),
        scratch_shapes=[pltpu.SemaphoreType.DMA((devices,))],
        compiler_params=pltpu.CompilerParams(vmem_limit_bytes=4 * 1024 * 1024),
        name="unpack",
    )(in_vmem(parts))


def on_device(volume, measured, cutoff):
    _, planes, pixels = volume.shape
    teams = lax.axis_size("frame")
    slabs = lax.axis_size("slab")
    mine = lax.axis_index("frame")
    length = planes * slabs
    width = pixels // (teams * slabs)
    axes = ("slab", "frame")

    columns = pack(volume[0], teams * slabs)
    columns = lax.all_to_all(columns, axes, split_axis=0, concat_axis=0, tiled=True)

    known = []
    own_tables = measured_tables(length)
    for shift in range(teams - 1, -1, -1):
        start = lax.rem(mine + shift, teams) * width
        part = measured_part(
            lax.dynamic_slice_in_dim(measured[0], start, width, axis=2),
            lax.dynamic_slice_in_dim(cutoff, start, width, axis=1),
            own_tables,
        )
        if shift:
            part = lax.ppermute(part, "frame", [(t, (t + shift) % teams) for t in range(teams)])
        known.insert(0, part)

    columns = columns.reshape(slabs, teams, planes, width)
    done = restore(mine.reshape(1), columns, known, band_tables(length))
    done = done.reshape(teams * slabs, planes, width)
    done = lax.all_to_all(done, axes, split_axis=0, concat_axis=0, tiled=True)
    return unpack(done)[None]


def solution(mesh):
    placed = (P("frame", "slab", None), P("frame", None, None, "slab"), P("frame", "slab"))
    return jax.shard_map(
        on_device, mesh=mesh, in_specs=placed, out_specs=P("frame", "slab", None), check_vma=False
    )
```

```python
import functools
import math

import jax
import jax.numpy as jnp
import numpy as np
from jax import lax
from jax.experimental import pallas as pl
from jax.experimental.pallas import tpu as pltpu
from jax.sharding import PartitionSpec as P


tv_step_size = 0.25
tv_weight = 1.0
EXTRA = 8


def split(array):
    high = array.astype(jnp.bfloat16)
    low = (array - high.astype(jnp.float32)).astype(jnp.bfloat16)
    return high, low


def product(table_high, table_low, array):
    high, low = split(array)
    tables = [table_high[...], table_high[...], table_low[...]]
    return jnp.dot(
        jnp.concatenate(tables, axis=1),
        jnp.concatenate([high, low, high], axis=0),
        preferred_element_type=jnp.float32,
    )


def in_vmem(array):
    return pltpu.with_memory_space_constraint(array, pltpu.VMEM)


def in_hbm(array):
    return pltpu.with_memory_space_constraint(array, pltpu.HBM)


def as_pair(table):
    table = table.astype(np.float32)
    high = table.astype(jnp.bfloat16)
    low = (table - high.astype(np.float32)).astype(jnp.bfloat16)
    return [jnp.asarray(high), jnp.asarray(low)]


def rows(length, first, count):
    k = first + 2 * np.arange(count)
    z = np.arange(length // 2)
    angle = (k[:, None] * z[None, :] % length) * (2.0 * math.pi / length)
    table = np.concatenate([np.cos(angle), -np.sin(angle)], axis=0) / math.sqrt(length)
    return k, table


def band_tables(length):
    count = 3 * length // 16
    result = []
    for first in (length // 8 + 2, length // 8 + 1):
        k, table = rows(length, first, count)
        weight = np.where(k == length // 2, 1.0, 2.0)
        result += as_pair(table * np.concatenate([weight, weight])[:, None])
        result += as_pair(table.T)
    return result


def measured_tables(length):
    result = []
    for first in (0, 1):
        result += as_pair(rows(length, first, length // 2)[1].T)
    return result


def measured_kernel(measured, cutoff, even_high, even_low, odd_high, odd_low, out):
    length = measured.shape[1]
    half = length // 2
    limit = cutoff[...]
    parts = []
    for first, high, low in ((0, even_high, even_low), (1, odd_high, odd_low)):
        k = first + 2 * lax.broadcasted_iota(jnp.int32, (half, limit.shape[1]), 0)
        keep = jnp.where(k < half, k, length - k) <= limit
        stacked = [
            jnp.where(keep, measured[part, pl.ds(first, half, stride=2), :], 0.0) for part in (0, 1)
        ]
        parts.append(product(high, low, jnp.concatenate(stacked, axis=0)))
    out[:half, :] = parts[0] + parts[1]
    out[half:length, :] = parts[0] - parts[1]
    out[length:, :] = jnp.broadcast_to(limit.astype(jnp.float32), (EXTRA, limit.shape[1]))


def measured_part(measured, cutoff, tables, order, width):
    length = measured.shape[1]
    count = measured.shape[2] // width
    whole = pl.BlockSpec(memory_space=pltpu.VMEM)
    if width % 128:
        measured = measured.reshape(2, length, count, width).transpose(2, 0, 1, 3)
        field = pl.BlockSpec((None, 2, length, width), lambda i, order: (order[i], 0, 0, 0))
        cutoff = cutoff.reshape(count, 1, width)
        limit = pl.BlockSpec((None, 1, width), lambda i, order: (order[i], 0, 0))
    else:
        field = pl.BlockSpec((2, length, width), lambda i, order: (0, 0, order[i]))
        limit = pl.BlockSpec((1, width), lambda i, order: (0, order[i]))
    return pl.pallas_call(
        lambda order, *refs: measured_kernel(*refs),
        grid_spec=pltpu.PrefetchScalarGridSpec(
            num_scalar_prefetch=1,
            grid=(count,),
            in_specs=[field, limit] + [whole] * len(tables),
            out_specs=pl.BlockSpec((None, length + EXTRA, width), lambda i, order: (i, 0, 0)),
        ),
        out_shape=jax.ShapeDtypeStruct((count, length + EXTRA, width), jnp.float32),
        compiler_params=pltpu.CompilerParams(vmem_limit_bytes=32 * 1024 * 1024),
        name="measured_part",
    )(order, in_hbm(measured), cutoff, *map(in_hbm, tables))


def start_fetches(sources, targets, sems, first):
    copies = [
        pltpu.make_async_copy(source, target, sems.at[first + i])
        for i, (source, target) in enumerate(zip(sources, targets))
    ]
    for copy in copies:
        copy.start()
    return copies


def wait_all(copies):
    for copy in copies:
        copy.wait()


def kept_band(halves, limits, tables, table_copies, known_copies):
    half = halves[0][0].shape[0]
    count = tables[0].shape[0] // 2
    result = []
    for side, first in ((0, half // 4 + 2), (1, half // 4 + 1)):
        wait_all(table_copies[4 * side : 4 * side + 2])
        spectra = [
            product(
                tables[4 * side],
                tables[4 * side + 1],
                low + high if side == 0 else low - high,
            )
            for low, high in halves
        ]
        if side == 0:
            wait_all(known_copies)
        wait_all(table_copies[4 * side + 2 : 4 * side + 4])
        parts = []
        for spectrum, limit in zip(spectra, limits):
            index = lax.broadcasted_iota(jnp.int32, spectrum.shape, 0)
            k = (first + 2 * jnp.where(index < count, index, index - count)).astype(jnp.float32)
            spectrum = jnp.where(k > limit(), spectrum, 0.0)
            parts.append(product(tables[4 * side + 2], tables[4 * side + 3], spectrum))
        result.append(parts)
    return result


def restore_kernel(mine, columns, *refs):
    slabs, frames, planes, width = columns.shape
    length = slabs * planes
    half = length // 2
    known_refs, table_refs, result = refs[:frames], refs[frames : frames + 8], refs[frames + 8]
    tables, known, out, sems = refs[frames + 9 : frames + 17], refs[-3], refs[-2], refs[-1]
    stores = []
    table_copies = start_fetches(table_refs, tables, sems, frames)
    known_copies = start_fetches(known_refs, [known.at[f] for f in range(frames)], sems, 0)
    where = [lax.rem(mine[0] + frames - shift, frames) for shift in range(frames)]
    pair = frames == 2 and width == 128

    def lanes(pieces):
        return [jnp.concatenate(pieces, axis=1)] if pair else pieces

    low = lanes([columns[: slabs // 2, f].reshape(half, width) for f in where])
    high = lanes([columns[slabs // 2 :, f].reshape(half, width) for f in where])

    def limit(shift):
        return known[shift, length : length + 1, :]

    if pair:
        limits = [lambda: lanes([limit(0), limit(1)])[0]]
    else:
        limits = [functools.partial(limit, shift) for shift in range(frames)]
    parts = kept_band(list(zip(low, high)), limits, tables, table_copies, known_copies)
    if pair:
        parts = [[part[0][:, :width], part[0][:, width:]] for part in parts]
    for i in range(half // planes):
        at = slice(i * planes, (i + 1) * planes)
        for side in (0, 1):
            anchor = []
            for shift in range(frames):
                even, odd = parts[0][shift][at, :], parts[1][shift][at, :]
                here = slice(side * half + i * planes, side * half + (i + 1) * planes)
                anchor.append(known[shift, here, :] + (even + odd if side == 0 else even - odd))
            place = side * (slabs // 2) + i
            values = smooth_two(anchor) if frames == 2 else anchor
            for f, value in zip(where, values):
                out[place, f] = value
            if frames == 2:
                stores += start_fetches(
                    [out.at[place]], [result.at[place]], sems, frames + 8 + place
                )
    if frames == 2:
        wait_all(stores)
    else:

        def smooth(i, carry):
            for f, value in enumerate(smooth_all([out[i, f] for f in range(frames)])):
                out[i, f] = value
            return carry

        lax.fori_loop(0, slabs, smooth, 0)


def smooth_two(anchor):
    d = anchor[1] - anchor[0]
    first = d * lax.rsqrt(d * d + 1.0)
    d = d - (2.0 * tv_step_size * tv_weight) * first
    second = d * lax.rsqrt(d * d + 1.0)
    move = (tv_step_size * tv_weight) * ((1.0 - tv_step_size) * first + second)
    return anchor[0] + move, anchor[1] - move


def smooth_all(anchor):
    frames = len(anchor)
    current = anchor
    for _ in range(2):
        fluxes = []
        for f in range(frames - 1):
            d = current[f + 1] - current[f]
            fluxes.append(d * lax.rsqrt(d * d + 1.0))
        following = []
        for f in range(frames):
            flow = 0.0
            if f > 0:
                flow = flow + fluxes[f - 1]
            if f < frames - 1:
                flow = flow - fluxes[f]
            following.append(
                current[f] - tv_step_size * ((current[f] - anchor[f]) + tv_weight * flow)
            )
        current = following
    return current


def restore(mine, columns, known, tables):
    whole = pl.BlockSpec(memory_space=pltpu.VMEM)
    hbm = pl.BlockSpec(memory_space=pltpu.HBM)
    return pl.pallas_call(
        restore_kernel,
        in_specs=[pl.BlockSpec(memory_space=pltpu.SMEM), whole]
        + [hbm] * (len(known) + len(tables)),
        out_specs=hbm,
        out_shape=pltpu.HBM(columns.shape, jnp.float32),
        scratch_shapes=[pltpu.VMEM(table.shape, table.dtype) for table in tables]
        + [
            pltpu.VMEM((len(known),) + known[0].shape, jnp.float32),
            pltpu.VMEM(columns.shape, jnp.float32),
            pltpu.SemaphoreType.DMA((len(known) + len(tables) + columns.shape[0],)),
        ],
        compiler_params=pltpu.CompilerParams(vmem_limit_bytes=24 * 1024 * 1024),
        name="restore",
    )(mine, in_vmem(columns), *map(in_hbm, known), *map(in_hbm, tables))


def anchor_kernel(slab, *refs):
    pieces = len(refs) - 21
    piece_refs, known_ref, table_refs = refs[:pieces], refs[pieces], refs[pieces + 1 : pieces + 9]
    out, tables = refs[pieces + 9], refs[pieces + 10 : pieces + 18]
    columns, known, sems = refs[-3:]
    half = out.shape[0] // 2
    width = out.shape[1]
    piece_copies = start_fetches(
        piece_refs, [columns.at[slab[0] ^ d] for d in range(pieces)], sems, 9
    )
    table_copies = start_fetches(table_refs, tables, sems, 1)
    blocks, _, block = known_ref.shape
    first = blocks - width // block
    known_copies = start_fetches(
        [known_ref.at[b] for b in range(first, blocks)],
        [known.at[:, pl.ds((b - first) * block, block)] for b in range(first, blocks)],
        sems,
        9 + pieces,
    )
    wait_all(piece_copies)
    low = columns[: pieces // 2].reshape(half, width)
    high = columns[pieces // 2 :].reshape(half, width)
    (even,), (odd,) = kept_band(
        [(low, high)],
        [lambda: known[2 * half : 2 * half + 1, :]],
        tables,
        table_copies,
        known_copies,
    )
    out[:half, :] = known[:half, :] + (even + odd)
    out[half:, :] = known[half : 2 * half, :] + (even - odd)


def anchor_of(slab, pieces, known, tables):
    whole = pl.BlockSpec(memory_space=pltpu.VMEM)
    hbm = pl.BlockSpec(memory_space=pltpu.HBM)
    planes, width = pieces[0].shape
    return pl.pallas_call(
        anchor_kernel,
        in_specs=[pl.BlockSpec(memory_space=pltpu.SMEM)]
        + [whole] * len(pieces)
        + [hbm] * (1 + len(tables)),
        out_specs=whole,
        out_shape=jax.ShapeDtypeStruct((len(pieces) * planes, width), jnp.float32),
        scratch_shapes=[pltpu.VMEM(table.shape, table.dtype) for table in tables]
        + [
            pltpu.VMEM((len(pieces), planes, width), jnp.float32),
            pltpu.VMEM((known.shape[1], width), jnp.float32),
            pltpu.SemaphoreType.DMA((1 + len(tables) + len(pieces) + width // known.shape[2],)),
        ],
        compiler_params=pltpu.CompilerParams(vmem_limit_bytes=24 * 1024 * 1024),
        name="anchor",
    )(slab, *map(in_vmem, pieces), in_hbm(known), *map(in_hbm, tables))


def smooth_kernel(slab, own, other, *outs):
    planes = outs[0].shape[0]
    for d, out in enumerate(outs):
        at = pl.ds(pl.multiple_of((slab[0] ^ d) * planes, planes), planes)
        out[...] = smooth_two([own[at, :], other[at, :]])[0]


def smooth_pieces(slab, own, other, count):
    whole = pl.BlockSpec(memory_space=pltpu.VMEM)
    length, width = own.shape
    return pl.pallas_call(
        smooth_kernel,
        in_specs=[pl.BlockSpec(memory_space=pltpu.SMEM), whole, whole],
        out_specs=[whole] * count,
        out_shape=[jax.ShapeDtypeStruct((length // count, width), jnp.float32)] * count,
        compiler_params=pltpu.CompilerParams(vmem_limit_bytes=8 * 1024 * 1024),
        name="smooth",
    )(slab, own, other)


def pack_split_kernel(slab, field, *refs):
    outs = refs[:-6]
    rows, held, pieces, here, there, everywhere = refs[-6:]
    direct, piece_outs = outs[0], outs[1:]
    strips, strip, _ = rows.shape
    devices, _, width = direct.shape
    piece = pieces.shape[2]
    at = [pl.ds(i * strip, strip) for i in range(strips)]
    loads = start_fetches([field.at[a, :] for a in at], [rows.at[i] for i in range(strips)], here, 0)
    stores = []
    for i in range(strips):
        loads[i].wait()
        for d in range(devices):
            first = (d // 2) * 2 * piece + (d % 2) * width
            held[i, d] = rows[i, :, first : first + width]
        stores += start_fetches([held.at[i]], [direct.at[:, at[i], :]], there, i)
        for d in range(len(piece_outs)):
            first = pl.multiple_of((slab[0] ^ d) * (2 * piece) + piece, 128)
            pieces[d, i * strip : (i + 1) * strip, :] = rows[i, :, pl.ds(first, piece)]
    stores += start_fetches(
        [pieces.at[d] for d in range(len(piece_outs))], piece_outs, everywhere, 0
    )
    wait_all(stores)


def pack_split(slab, field, slabs):
    planes, pixels = field.shape
    piece = pixels // slabs // 2
    strips = planes // 16
    hbm = pl.BlockSpec(memory_space=pltpu.HBM)
    return pl.pallas_call(
        pack_split_kernel,
        in_specs=[pl.BlockSpec(memory_space=pltpu.SMEM), hbm],
        out_specs=[hbm] * (1 + slabs),
        out_shape=[pltpu.HBM((2 * slabs, planes, piece // 2), jnp.float32)]
        + [pltpu.HBM((planes, piece), jnp.float32)] * slabs,
        scratch_shapes=[
            pltpu.VMEM((strips, 16, pixels), jnp.float32),
            pltpu.VMEM((strips, 2 * slabs, 16, piece // 2), jnp.float32),
            pltpu.VMEM((slabs, planes, piece), jnp.float32),
            pltpu.SemaphoreType.DMA((strips,)),
            pltpu.SemaphoreType.DMA((strips,)),
            pltpu.SemaphoreType.DMA((slabs,)),
        ],
        compiler_params=pltpu.CompilerParams(vmem_limit_bytes=8 * 1024 * 1024),
        name="pack_split",
    )(slab, in_hbm(field))


def unpack_split_kernel(slab, direct, *refs):
    pieces, out, sems = refs[:-2], refs[-2], refs[-1]
    devices, _, width = direct.shape
    sources = [direct.at[d] for d in range(devices)] + list(pieces)
    piece = 2 * width
    targets = [
        out.at[:, pl.ds((d // 2) * 2 * piece + (d % 2) * width, width)] for d in range(devices)
    ]
    for d in range(len(pieces)):
        first = pl.multiple_of((slab[0] ^ d) * (2 * piece) + piece, 128)
        targets.append(out.at[:, pl.ds(first, piece)])
    wait_all(start_fetches(sources, targets, sems, 0))


def unpack_split(slab, direct, pieces):
    hbm = pl.BlockSpec(memory_space=pltpu.HBM)
    devices, planes, width = direct.shape
    return pl.pallas_call(
        unpack_split_kernel,
        in_specs=[pl.BlockSpec(memory_space=pltpu.SMEM)]
        + [pl.BlockSpec(memory_space=pltpu.VMEM)] * (1 + len(pieces)),
        out_specs=hbm,
        out_shape=jax.ShapeDtypeStruct((planes, 2 * devices * width), jnp.float32),
        scratch_shapes=[pltpu.SemaphoreType.DMA((devices + len(pieces),))],
        compiler_params=pltpu.CompilerParams(vmem_limit_bytes=4 * 1024 * 1024),
        name="unpack_split",
    )(slab, in_vmem(direct), *map(in_vmem, pieces))


def pack_kernel(field, out, rows, held, here, there):
    strips, strip, _ = rows.shape
    devices, _, width = out.shape
    at = [pl.ds(i * strip, strip) for i in range(strips)]
    loads = [
        pltpu.make_async_copy(field.at[at[i], :], rows.at[i], here.at[i]) for i in range(strips)
    ]
    stores = [
        pltpu.make_async_copy(held.at[i], out.at[:, at[i], :], there.at[i]) for i in range(strips)
    ]
    for load in loads:
        load.start()
    for i in range(strips):
        loads[i].wait()
        for d in range(devices):
            held[i, d] = rows[i, :, d * width : (d + 1) * width]
        stores[i].start()
    for store in stores:
        store.wait()


def pack(field, devices):
    planes, pixels = field.shape
    width = pixels // devices
    if width % 128:
        return field.reshape(planes, devices, width).transpose(1, 0, 2)
    strips = planes // 16
    return pl.pallas_call(
        pack_kernel,
        in_specs=[pl.BlockSpec(memory_space=pltpu.HBM)],
        out_specs=pl.BlockSpec(memory_space=pltpu.HBM),
        out_shape=pltpu.HBM((devices, planes, width), jnp.float32),
        scratch_shapes=[
            pltpu.VMEM((strips, 16, pixels), jnp.float32),
            pltpu.VMEM((strips, devices, 16, width), jnp.float32),
            pltpu.SemaphoreType.DMA((strips,)),
            pltpu.SemaphoreType.DMA((strips,)),
        ],
        compiler_params=pltpu.CompilerParams(vmem_limit_bytes=8 * 1024 * 1024),
        name="pack",
    )(in_hbm(field))


def unpack_kernel(parts, out, sems):
    devices, _, width = parts.shape
    copies = [
        pltpu.make_async_copy(parts.at[i], out.at[:, pl.ds(i * width, width)], sems.at[i])
        for i in range(devices)
    ]
    for copy in copies:
        copy.start()
    for copy in copies:
        copy.wait()


def unpack(parts):
    devices, planes, width = parts.shape
    if width % 128:
        return parts.transpose(1, 0, 2).reshape(planes, devices * width)
    return pl.pallas_call(
        unpack_kernel,
        in_specs=[pl.BlockSpec(memory_space=pltpu.VMEM)],
        out_specs=pl.BlockSpec(memory_space=pltpu.HBM),
        out_shape=jax.ShapeDtypeStruct((planes, devices * width), jnp.float32),
        scratch_shapes=[pltpu.SemaphoreType.DMA((devices,))],
        compiler_params=pltpu.CompilerParams(vmem_limit_bytes=4 * 1024 * 1024),
        name="unpack",
    )(in_vmem(parts))


def exchange(blocks):
    return lax.all_to_all(blocks, ("slab", "frame"), split_axis=0, concat_axis=0, tiled=True)


def known_parts(measured, cutoff, width):
    teams = lax.axis_size("frame")
    mine = lax.axis_index("frame")
    count = measured.shape[3] // width
    order = lax.rem(mine + jnp.arange(teams, dtype=jnp.int32), teams)
    order = jnp.concatenate([order, jnp.arange(teams, count, dtype=jnp.int32)])
    blocks = measured_part(measured[0], cutoff, measured_tables(measured.shape[2]), order, width)
    known = [blocks[0]]
    for shift in range(1, teams):
        pairs = [(t, (t + shift) % teams) for t in range(teams)]
        known.append(lax.ppermute(blocks[shift], "frame", pairs))
    return known, blocks


def on_device(volume, measured, cutoff):
    _, planes, pixels = volume.shape
    teams = lax.axis_size("frame")
    slabs = lax.axis_size("slab")
    mine = lax.axis_index("frame").reshape(1)
    length = planes * slabs
    if teams == 2 and slabs & (slabs - 1) == 0 and pixels % (512 * slabs) == 0:
        return split_on_device(volume, measured, cutoff)
    width = pixels // (teams * slabs)
    columns = exchange(pack(volume[0], teams * slabs))
    known, _ = known_parts(measured, cutoff, width)
    columns = columns.reshape(slabs, teams, planes, width)
    done = restore(mine, columns, known, band_tables(length))
    return unpack(exchange(done.reshape(teams * slabs, planes, width)))[None]


def permute(piece, distance):
    if distance == 0:
        return piece
    slabs = lax.axis_size("slab")
    return lax.ppermute(piece, "slab", [(s, s ^ distance) for s in range(slabs)])


def split_on_device(volume, measured, cutoff):
    _, planes, pixels = volume.shape
    slabs = lax.axis_size("slab")
    mine = lax.axis_index("frame").reshape(1)
    slab = lax.axis_index("slab").reshape(1)
    length = planes * slabs
    piece = pixels // slabs // 2
    width = piece // 2
    tables = band_tables(length)

    direct, *pieces = pack_split(slab, volume[0], slabs)
    columns = exchange(direct)
    order = sorted(range(slabs), key=lambda d: -d)
    arrived = [None] * slabs
    for d in order:
        arrived[d] = permute(pieces[d], d)

    known, blocks = known_parts(measured, cutoff, width)

    done = restore(mine, columns.reshape(slabs, 2, planes, width), known, tables)
    direct = exchange(done.reshape(2 * slabs, planes, width))

    anchor = anchor_of(slab, arrived, blocks, tables)
    other = lax.ppermute(anchor, "frame", [(0, 1), (1, 0)])
    pieces = smooth_pieces(slab, anchor, other, slabs)
    arrived = [None] * slabs
    for d in order:
        arrived[d] = permute(pieces[d], d)
    return unpack_split(slab, direct, arrived)[None]


def solution(mesh):
    placed = (P("frame", "slab", None), P("frame", None, None, "slab"), P("frame", "slab"))

    return jax.shard_map(
        on_device, mesh=mesh, in_specs=placed, out_specs=P("frame", "slab", None), check_vma=False
    )
```

```python
import functools
import math

import jax
import jax.numpy as jnp
import numpy as np
from jax import lax
from jax.experimental import pallas as pl
from jax.experimental.pallas import tpu as pltpu
from jax.sharding import PartitionSpec as P


tv_step_size = 0.25
tv_weight = 1.0
EXTRA = 8


def split(array):
    high = array.astype(jnp.bfloat16)
    low = (array - high.astype(jnp.float32)).astype(jnp.bfloat16)
    return high, low


def product(table_high, table_low, array):
    high, low = split(array)
    tables = [table_high[...], table_high[...], table_low[...]]
    return jnp.dot(
        jnp.concatenate(tables, axis=1),
        jnp.concatenate([high, low, high], axis=0),
        preferred_element_type=jnp.float32,
    )


def in_vmem(array):
    return pltpu.with_memory_space_constraint(array, pltpu.VMEM)


def in_hbm(array):
    return pltpu.with_memory_space_constraint(array, pltpu.HBM)


def as_pair(table):
    table = table.astype(np.float32)
    high = table.astype(jnp.bfloat16)
    low = (table - high.astype(np.float32)).astype(jnp.bfloat16)
    return [jnp.asarray(high), jnp.asarray(low)]


def rows(length, first, count):
    k = first + 2 * np.arange(count)
    z = np.arange(length // 2)
    angle = (k[:, None] * z[None, :] % length) * (2.0 * math.pi / length)
    table = np.concatenate([np.cos(angle), -np.sin(angle)], axis=0) / math.sqrt(length)
    return k, table


def band_tables(length):
    count = 3 * length // 16
    result = []
    for first in (length // 8 + 2, length // 8 + 1):
        k, table = rows(length, first, count)
        weight = np.where(k == length // 2, 1.0, 2.0)
        result += as_pair(table * np.concatenate([weight, weight])[:, None])
        result += as_pair(table.T)
    return result


def measured_tables(length):
    count = 3 * length // 16
    result = []
    for first in (0, 1):
        low = rows(length, first, count)[1]
        high = rows(length, 5 * length // 8 + first, count)[1]
        parts = [low[:count], high[:count], low[count:], high[count:]]
        result += as_pair(np.concatenate(parts, axis=0).T)
    return result


def measured_kernel(measured, cutoff, even_high, even_low, odd_high, odd_low, out):
    length = measured.shape[1]
    half = length // 2
    limit = cutoff[...]
    count = 3 * length // 16
    edge = 3 * length // 8
    parts = []
    for first, high, low in ((0, even_high, even_low), (1, odd_high, odd_low)):
        row = lax.broadcasted_iota(jnp.int32, (count, limit.shape[1]), 0)
        k = first + 2 * row
        stacked = []
        for part in (0, 1):
            below = measured[part, pl.ds(first, count, stride=2), :]
            above = measured[part, pl.ds(length - edge + first, count, stride=2), :]
            above = jnp.where(edge - k <= limit, above, 0.0)
            if first == 0:
                last = jnp.where(edge <= limit, measured[part, edge : edge + 1, :], 0.0)
                joined = above + last if part == 0 else above - last
                above = jnp.where(row == 0, joined, above)
            stacked += [jnp.where(k <= limit, below, 0.0), above]
        parts.append(product(high, low, jnp.concatenate(stacked, axis=0)))
    out[:half, :] = parts[0] + parts[1]
    out[half:length, :] = parts[0] - parts[1]
    out[length:, :] = jnp.broadcast_to(limit.astype(jnp.float32), (EXTRA, limit.shape[1]))


def measured_part(measured, cutoff, tables, order, width):
    length = measured.shape[1]
    count = measured.shape[2] // width
    whole = pl.BlockSpec(memory_space=pltpu.VMEM)
    if width % 128:
        measured = measured.reshape(2, length, count, width).transpose(2, 0, 1, 3)
        field = pl.BlockSpec((None, 2, length, width), lambda i, order: (order[i], 0, 0, 0))
        cutoff = cutoff.reshape(count, 1, width)
        limit = pl.BlockSpec((None, 1, width), lambda i, order: (order[i], 0, 0))
    else:
        field = pl.BlockSpec((2, length, width), lambda i, order: (0, 0, order[i]))
        limit = pl.BlockSpec((1, width), lambda i, order: (0, order[i]))
    return pl.pallas_call(
        lambda order, *refs: measured_kernel(*refs),
        grid_spec=pltpu.PrefetchScalarGridSpec(
            num_scalar_prefetch=1,
            grid=(count,),
            in_specs=[field, limit] + [whole] * len(tables),
            out_specs=pl.BlockSpec((None, length + EXTRA, width), lambda i, order: (i, 0, 0)),
        ),
        out_shape=jax.ShapeDtypeStruct((count, length + EXTRA, width), jnp.float32),
        compiler_params=pltpu.CompilerParams(vmem_limit_bytes=32 * 1024 * 1024),
        name="measured_part",
    )(order, in_hbm(measured), cutoff, *map(in_hbm, tables))


def start_fetches(sources, targets, sems, first):
    copies = [
        pltpu.make_async_copy(source, target, sems.at[first + i])
        for i, (source, target) in enumerate(zip(sources, targets))
    ]
    for copy in copies:
        copy.start()
    return copies


def wait_all(copies):
    for copy in copies:
        copy.wait()


def kept_band(halves, limits, tables, table_copies, known_copies):
    half = halves[0][0].shape[0]
    count = tables[0].shape[0] // 2
    result = []
    for side, first in ((0, half // 4 + 2), (1, half // 4 + 1)):
        wait_all(table_copies[4 * side : 4 * side + 2])
        spectra = [
            product(
                tables[4 * side],
                tables[4 * side + 1],
                low + high if side == 0 else low - high,
            )
            for low, high in halves
        ]
        if side == 0:
            wait_all(known_copies)
        wait_all(table_copies[4 * side + 2 : 4 * side + 4])
        parts = []
        for spectrum, limit in zip(spectra, limits):
            index = lax.broadcasted_iota(jnp.int32, spectrum.shape, 0)
            k = (first + 2 * jnp.where(index < count, index, index - count)).astype(jnp.float32)
            spectrum = jnp.where(k > limit(), spectrum, 0.0)
            parts.append(product(tables[4 * side + 2], tables[4 * side + 3], spectrum))
        result.append(parts)
    return result


def restore_kernel(mine, columns, *refs):
    slabs, frames, planes, width = columns.shape
    length = slabs * planes
    half = length // 2
    known_refs, table_refs, result = refs[:frames], refs[frames : frames + 8], refs[frames + 8]
    known, out, sems = refs[-3:]
    fetched = refs[frames + 9 : -3]
    tables = fetched
    stores = []
    table_copies = start_fetches(table_refs, fetched, sems, frames)
    known_copies = start_fetches(known_refs, [known.at[f] for f in range(frames)], sems, 0)
    where = [lax.rem(mine[0] + frames - shift, frames) for shift in range(frames)]
    pair = frames == 2 and width == 128

    def lanes(pieces):
        return [jnp.concatenate(pieces, axis=1)] if pair else pieces

    low = lanes([columns[: slabs // 2, f].reshape(half, width) for f in where])
    high = lanes([columns[slabs // 2 :, f].reshape(half, width) for f in where])

    def limit(shift):
        return known[shift, length : length + 1, :]

    if pair:
        limits = [lambda: lanes([limit(0), limit(1)])[0]]
    else:
        limits = [functools.partial(limit, shift) for shift in range(frames)]
    parts = kept_band(list(zip(low, high)), limits, tables, table_copies, known_copies)
    if pair:
        parts = [[part[0][:, :width], part[0][:, width:]] for part in parts]
    for i in range(half // planes):
        at = slice(i * planes, (i + 1) * planes)
        for side in (0, 1):
            anchor = []
            for shift in range(frames):
                even, odd = parts[0][shift][at, :], parts[1][shift][at, :]
                here = slice(side * half + i * planes, side * half + (i + 1) * planes)
                anchor.append(known[shift, here, :] + (even + odd if side == 0 else even - odd))
            place = side * (slabs // 2) + i
            values = smooth_two(anchor) if frames == 2 else anchor
            for f, value in zip(where, values):
                out[place, f] = value
            if frames == 2:
                stores += start_fetches(
                    [out.at[place]], [result.at[place]], sems, frames + 8 + place
                )
    if frames == 2:
        wait_all(stores)
    else:

        def smooth(i, carry):
            for f, value in enumerate(smooth_all([out[i, f] for f in range(frames)])):
                out[i, f] = value
            return carry

        lax.fori_loop(0, slabs, smooth, 0)


def smooth_two(anchor):
    d = anchor[1] - anchor[0]
    first = d * lax.rsqrt(d * d + 1.0)
    d = d - (2.0 * tv_step_size * tv_weight) * first
    second = d * lax.rsqrt(d * d + 1.0)
    move = (tv_step_size * tv_weight) * ((1.0 - tv_step_size) * first + second)
    return anchor[0] + move, anchor[1] - move


def smooth_all(anchor):
    frames = len(anchor)
    current = anchor
    for _ in range(2):
        fluxes = []
        for f in range(frames - 1):
            d = current[f + 1] - current[f]
            fluxes.append(d * lax.rsqrt(d * d + 1.0))
        following = []
        for f in range(frames):
            flow = 0.0
            if f > 0:
                flow = flow + fluxes[f - 1]
            if f < frames - 1:
                flow = flow - fluxes[f]
            following.append(
                current[f] - tv_step_size * ((current[f] - anchor[f]) + tv_weight * flow)
            )
        current = following
    return current


def restore(mine, columns, known, tables):
    whole = pl.BlockSpec(memory_space=pltpu.VMEM)
    hbm = pl.BlockSpec(memory_space=pltpu.HBM)
    return pl.pallas_call(
        restore_kernel,
        in_specs=[pl.BlockSpec(memory_space=pltpu.SMEM), whole]
        + [hbm] * len(known)
        + [hbm] * len(tables),
        out_specs=hbm,
        out_shape=pltpu.HBM(columns.shape, jnp.float32),
        scratch_shapes=[pltpu.VMEM(table.shape, table.dtype) for table in tables]
        + [
            pltpu.VMEM((len(known),) + known[0].shape, jnp.float32),
            pltpu.VMEM(columns.shape, jnp.float32),
            pltpu.SemaphoreType.DMA((len(known) + len(tables) + columns.shape[0],)),
        ],
        compiler_params=pltpu.CompilerParams(vmem_limit_bytes=24 * 1024 * 1024),
        name="restore",
    )(mine, in_vmem(columns), *map(in_hbm, known), *map(in_hbm, tables))


def anchor_kernel(slab, *refs):
    pieces = len(refs) - 21
    piece_refs, known_ref, table_refs = refs[:pieces], refs[pieces], refs[pieces + 1 : pieces + 9]
    out, fetched = refs[pieces + 9], refs[pieces + 10 : -3]
    tables = fetched
    columns, known, sems = refs[-3:]
    half = out.shape[0] // 2
    width = out.shape[1]
    piece_copies = start_fetches(
        piece_refs, [columns.at[slab[0] ^ d] for d in range(pieces)], sems, 9
    )
    table_copies = start_fetches(table_refs, fetched, sems, 1)
    blocks, _, block = known_ref.shape
    first = blocks - width // block
    known_copies = start_fetches(
        [known_ref.at[b] for b in range(first, blocks)],
        [known.at[:, pl.ds((b - first) * block, block)] for b in range(first, blocks)],
        sems,
        9 + pieces,
    )
    wait_all(piece_copies)
    low = columns[: pieces // 2].reshape(half, width)
    high = columns[pieces // 2 :].reshape(half, width)
    (even,), (odd,) = kept_band(
        [(low, high)],
        [lambda: known[2 * half : 2 * half + 1, :]],
        tables,
        table_copies,
        known_copies,
    )
    out[:half, :] = known[:half, :] + (even + odd)
    out[half:, :] = known[half : 2 * half, :] + (even - odd)


def anchor_of(slab, pieces, known, tables):
    whole = pl.BlockSpec(memory_space=pltpu.VMEM)
    hbm = pl.BlockSpec(memory_space=pltpu.HBM)
    planes, width = pieces[0].shape
    return pl.pallas_call(
        anchor_kernel,
        in_specs=[pl.BlockSpec(memory_space=pltpu.SMEM)]
        + [whole] * len(pieces)
        + [hbm]
        + [hbm] * len(tables),
        out_specs=whole,
        out_shape=jax.ShapeDtypeStruct((len(pieces) * planes, width), jnp.float32),
        scratch_shapes=[pltpu.VMEM(table.shape, table.dtype) for table in tables]
        + [
            pltpu.VMEM((len(pieces), planes, width), jnp.float32),
            pltpu.VMEM((known.shape[1], width), jnp.float32),
            pltpu.SemaphoreType.DMA((1 + len(tables) + len(pieces) + width // known.shape[2],)),
        ],
        compiler_params=pltpu.CompilerParams(vmem_limit_bytes=24 * 1024 * 1024),
        name="anchor",
    )(slab, *map(in_vmem, pieces), in_hbm(known), *map(in_hbm, tables))


def smooth_kernel(slab, own, other, *outs):
    planes = outs[0].shape[0]
    for d, out in enumerate(outs):
        at = pl.ds(pl.multiple_of((slab[0] ^ d) * planes, planes), planes)
        out[...] = smooth_two([own[at, :], other[at, :]])[0]


def smooth_pieces(slab, own, other, count):
    whole = pl.BlockSpec(memory_space=pltpu.VMEM)
    length, width = own.shape
    return pl.pallas_call(
        smooth_kernel,
        in_specs=[pl.BlockSpec(memory_space=pltpu.SMEM), whole, whole],
        out_specs=[whole] * count,
        out_shape=[jax.ShapeDtypeStruct((length // count, width), jnp.float32)] * count,
        compiler_params=pltpu.CompilerParams(vmem_limit_bytes=8 * 1024 * 1024),
        name="smooth",
    )(slab, own, other)


def pack_split_kernel(slab, field, *refs):
    outs = refs[:-6]
    rows, held, pieces, here, there, everywhere = refs[-6:]
    direct, piece_outs = outs[0], outs[1:]
    strips, strip, _ = rows.shape
    devices, _, width = direct.shape
    piece = pieces.shape[2]
    at = [pl.ds(i * strip, strip) for i in range(strips)]
    loads = start_fetches([field.at[a, :] for a in at], [rows.at[i] for i in range(strips)], here, 0)
    stores = []
    for i in range(strips):
        loads[i].wait()
        for d in range(devices):
            first = (d // 2) * 2 * piece + (d % 2) * width
            held[i, d] = rows[i, :, first : first + width]
        stores += start_fetches([held.at[i]], [direct.at[:, at[i], :]], there, i)
        for d in range(len(piece_outs)):
            first = pl.multiple_of((slab[0] ^ d) * (2 * piece) + piece, 128)
            pieces[d, i * strip : (i + 1) * strip, :] = rows[i, :, pl.ds(first, piece)]
    stores += start_fetches(
        [pieces.at[d] for d in range(len(piece_outs))], piece_outs, everywhere, 0
    )
    wait_all(stores)


def pack_split(slab, field, slabs):
    planes, pixels = field.shape
    piece = pixels // slabs // 2
    strips = planes // 16
    hbm = pl.BlockSpec(memory_space=pltpu.HBM)
    return pl.pallas_call(
        pack_split_kernel,
        in_specs=[pl.BlockSpec(memory_space=pltpu.SMEM), hbm],
        out_specs=[hbm] * (1 + slabs),
        out_shape=[pltpu.HBM((2 * slabs, planes, piece // 2), jnp.float32)]
        + [pltpu.HBM((planes, piece), jnp.float32)] * slabs,
        scratch_shapes=[
            pltpu.VMEM((strips, 16, pixels), jnp.float32),
            pltpu.VMEM((strips, 2 * slabs, 16, piece // 2), jnp.float32),
            pltpu.VMEM((slabs, planes, piece), jnp.float32),
            pltpu.SemaphoreType.DMA((strips,)),
            pltpu.SemaphoreType.DMA((strips,)),
            pltpu.SemaphoreType.DMA((slabs,)),
        ],
        compiler_params=pltpu.CompilerParams(vmem_limit_bytes=8 * 1024 * 1024),
        name="pack_split",
    )(slab, in_hbm(field))


def unpack_split_kernel(slab, direct, *refs):
    pieces, out, sems = refs[:-2], refs[-2], refs[-1]
    devices, _, width = direct.shape
    sources = [direct.at[d] for d in range(devices)] + list(pieces)
    piece = 2 * width
    targets = [
        out.at[:, pl.ds((d // 2) * 2 * piece + (d % 2) * width, width)] for d in range(devices)
    ]
    for d in range(len(pieces)):
        first = pl.multiple_of((slab[0] ^ d) * (2 * piece) + piece, 128)
        targets.append(out.at[:, pl.ds(first, piece)])
    wait_all(start_fetches(sources, targets, sems, 0))


def unpack_split(slab, direct, pieces):
    hbm = pl.BlockSpec(memory_space=pltpu.HBM)
    devices, planes, width = direct.shape
    return pl.pallas_call(
        unpack_split_kernel,
        in_specs=[pl.BlockSpec(memory_space=pltpu.SMEM)]
        + [pl.BlockSpec(memory_space=pltpu.VMEM)] * (1 + len(pieces)),
        out_specs=hbm,
        out_shape=jax.ShapeDtypeStruct((planes, 2 * devices * width), jnp.float32),
        scratch_shapes=[pltpu.SemaphoreType.DMA((devices + len(pieces),))],
        compiler_params=pltpu.CompilerParams(vmem_limit_bytes=4 * 1024 * 1024),
        name="unpack_split",
    )(slab, in_vmem(direct), *map(in_vmem, pieces))


def pack_kernel(field, out, rows, held, here, there):
    strips, strip, _ = rows.shape
    devices, _, width = out.shape
    at = [pl.ds(i * strip, strip) for i in range(strips)]
    loads = [
        pltpu.make_async_copy(field.at[at[i], :], rows.at[i], here.at[i]) for i in range(strips)
    ]
    stores = [
        pltpu.make_async_copy(held.at[i], out.at[:, at[i], :], there.at[i]) for i in range(strips)
    ]
    for load in loads:
        load.start()
    for i in range(strips):
        loads[i].wait()
        for d in range(devices):
            held[i, d] = rows[i, :, d * width : (d + 1) * width]
        stores[i].start()
    for store in stores:
        store.wait()


def pack(field, devices):
    planes, pixels = field.shape
    width = pixels // devices
    if width % 128:
        return field.reshape(planes, devices, width).transpose(1, 0, 2)
    strips = planes // 16
    return pl.pallas_call(
        pack_kernel,
        in_specs=[pl.BlockSpec(memory_space=pltpu.HBM)],
        out_specs=pl.BlockSpec(memory_space=pltpu.HBM),
        out_shape=pltpu.HBM((devices, planes, width), jnp.float32),
        scratch_shapes=[
            pltpu.VMEM((strips, 16, pixels), jnp.float32),
            pltpu.VMEM((strips, devices, 16, width), jnp.float32),
            pltpu.SemaphoreType.DMA((strips,)),
            pltpu.SemaphoreType.DMA((strips,)),
        ],
        compiler_params=pltpu.CompilerParams(vmem_limit_bytes=8 * 1024 * 1024),
        name="pack",
    )(in_hbm(field))


def unpack_kernel(parts, out, sems):
    devices, _, width = parts.shape
    copies = [
        pltpu.make_async_copy(parts.at[i], out.at[:, pl.ds(i * width, width)], sems.at[i])
        for i in range(devices)
    ]
    for copy in copies:
        copy.start()
    for copy in copies:
        copy.wait()


def unpack(parts):
    devices, planes, width = parts.shape
    if width % 128:
        return parts.transpose(1, 0, 2).reshape(planes, devices * width)
    return pl.pallas_call(
        unpack_kernel,
        in_specs=[pl.BlockSpec(memory_space=pltpu.VMEM)],
        out_specs=pl.BlockSpec(memory_space=pltpu.HBM),
        out_shape=jax.ShapeDtypeStruct((planes, devices * width), jnp.float32),
        scratch_shapes=[pltpu.SemaphoreType.DMA((devices,))],
        compiler_params=pltpu.CompilerParams(vmem_limit_bytes=4 * 1024 * 1024),
        name="unpack",
    )(in_vmem(parts))


def exchange(blocks):
    return lax.all_to_all(blocks, ("slab", "frame"), split_axis=0, concat_axis=0, tiled=True)


def known_parts(measured, cutoff, width):
    teams = lax.axis_size("frame")
    mine = lax.axis_index("frame")
    count = measured.shape[3] // width
    order = lax.rem(mine + jnp.arange(teams, dtype=jnp.int32), teams)
    order = jnp.concatenate([order, jnp.arange(teams, count, dtype=jnp.int32)])
    blocks = measured_part(measured[0], cutoff, measured_tables(measured.shape[2]), order, width)
    known = [blocks[0]]
    for shift in range(1, teams):
        pairs = [(t, (t + shift) % teams) for t in range(teams)]
        known.append(lax.ppermute(blocks[shift], "frame", pairs))
    return known, blocks


def on_device(volume, measured, cutoff):
    _, planes, pixels = volume.shape
    teams = lax.axis_size("frame")
    slabs = lax.axis_size("slab")
    mine = lax.axis_index("frame").reshape(1)
    length = planes * slabs
    if teams == 2 and slabs & (slabs - 1) == 0 and pixels % (512 * slabs) == 0:
        return split_on_device(volume, measured, cutoff)
    width = pixels // (teams * slabs)
    columns = exchange(pack(volume[0], teams * slabs))
    known, _ = known_parts(measured, cutoff, width)
    columns = columns.reshape(slabs, teams, planes, width)
    done = restore(mine, columns, known, band_tables(length))
    return unpack(exchange(done.reshape(teams * slabs, planes, width)))[None]


def permute(piece, distance):
    if distance == 0:
        return piece
    slabs = lax.axis_size("slab")
    return lax.ppermute(piece, "slab", [(s, s ^ distance) for s in range(slabs)])


def split_on_device(volume, measured, cutoff):
    _, planes, pixels = volume.shape
    slabs = lax.axis_size("slab")
    mine = lax.axis_index("frame").reshape(1)
    slab = lax.axis_index("slab").reshape(1)
    length = planes * slabs
    piece = pixels // slabs // 2
    width = piece // 2
    tables = band_tables(length)

    direct, *pieces = pack_split(slab, volume[0], slabs)
    columns = exchange(direct)
    order = sorted(range(slabs), key=lambda d: -d)
    arrived = [None] * slabs
    for d in order:
        arrived[d] = permute(pieces[d], d)

    known, blocks = known_parts(measured, cutoff, width)

    done = restore(mine, columns.reshape(slabs, 2, planes, width), known, tables)
    direct = exchange(done.reshape(2 * slabs, planes, width))

    anchor = anchor_of(slab, arrived, blocks, tables)
    other = lax.ppermute(anchor, "frame", [(0, 1), (1, 0)])
    pieces = smooth_pieces(slab, anchor, other, slabs)
    arrived = [None] * slabs
    for d in order:
        arrived[d] = permute(pieces[d], d)
    return unpack_split(slab, direct, arrived)[None]


def solution(mesh):
    placed = (P("frame", "slab", None), P("frame", None, None, "slab"), P("frame", "slab"))

    return jax.shard_map(
        on_device, mesh=mesh, in_specs=placed, out_specs=P("frame", "slab", None), check_vma=False
    )
```
